32 devices in a mesh: dp: 8 (over z, x), head: 4 (over y, core).
Axes of the slice: x: 2, y: 2, z: 4, core: 2. Of those that a mesh axis runs over, the one named last changes fastest.
Arguments:
- tokens: bfloat16 [8192, 1024], P(('dp', 'head')), may hold values from -6 to 6
- w_query: bfloat16 [1024, 1024], P(None, 'head'), may hold values from -0.1875 to 0.1875
- w_key: bfloat16 [1024, 1024], P(None, 'head'), may hold values from -0.1875 to 0.1875
- w_value: bfloat16 [1024, 1024], P(None, 'head'), may hold values from -0.1875 to 0.1875
- w_out: bfloat16 [1024, 1024], P('head'), may hold values from -0.375 to 0.375
- s_qk: float32 [1024], P('head'), may hold values from 1 to 1.7
- alpha_attn: float32 [1024], replicated, may hold values from 0.15 to 0.6
- w_gate: bfloat16 [1024, 4096], P(None, ('dp', 'head')), may hold values from -0.1875 to 0.1875
- w_up: bfloat16 [1024, 4096], P(None, ('dp', 'head')), may hold values from -0.1875 to 0.1875
- w_down: bfloat16 [1024, 4096], P(None, ('dp', 'head')), may hold values from -0.09375 to 0.09375
- s_gate: float32 [4096], P(('dp', 'head')), may hold values from 0.7 to 1.4
- s_up: float32 [4096], P(('dp', 'head')), may hold values from 0.7 to 1.4
- alpha_mlp: float32 [1024], replicated, may hold values from 0.15 to 0.6
- seq_ids: int32 [8192], P('dp'), may hold values from 0 to 1024, as said below
- counts: int32 [8], P('dp'), may hold values from 512 to 1024, as said below
- out_grad: float32 [8192, 1024], P(('dp', 'head')), may hold values from -6 to 6
Outputs:
- output: bfloat16 [8192, 1024], P(('dp', 'head'))
- grad_tokens: float32 [8192, 1024], P(('dp', 'head'))
- grad_w_query: float32 [1024, 1024], P(None, 'head')
- grad_w_key: float32 [1024, 1024], P(None, 'head')
- grad_w_value: float32 [1024, 1024], P(None, 'head')
- grad_w_out: float32 [1024, 1024], P('head')
- grad_s_qk: float32 [1024], P('head')
- grad_alpha_attn: float32 [1024], replicated
- grad_w_gate: float32 [1024, 4096], P(None, ('dp', 'head'))
- grad_w_up: float32 [1024, 4096], P(None, ('dp', 'head'))
- grad_w_down: float32 [1024, 4096], P(None, ('dp', 'head'))
- grad_s_gate: float32 [4096], P(('dp', 'head'))
- grad_s_up: float32 [4096], P(('dp', 'head'))
- grad_alpha_mlp: float32 [1024], replicated
- grad_norm: float32 [], replicated
- mean_alpha: float32 [], replicated
The draws below stay inside these ranges and needn't reach their ends.
Inputs may be any that keep to these rules, and one draw needn't show every extreme that they name: `seq_ids`: within each block of 1024 slots the ids start at 0 and never fall; every document has 512 to 1024 tokens; the slots after a block's last document carry the id 1024; one block holds a single document of 1024 tokens. counts[g] is the number of slots of block g whose id is under 1024.
All inputs are finite; a program needn't handle non-finite values.
Results may differ from the reference program's by a relative error of at most 0.025.
Values may be sent and summed in bfloat16 or wider, within the bound.
No kernel may reach another device: no remote copies, remote signals or barrier semaphores. Data moves between devices by JAX's collectives and lax.ppermute only.
A program may use at most 256 MiB of HBM per device.

```python
import math
import jax
import jax.numpy as jnp
from jax import lax

D = 1024
HEADS = 16
HEAD_DIM = 64
FF = 4096
GROUP = 1024
SEQ_SHORT = 512
TOKENS = 8192


def packing(key):
    group_count = TOKENS // GROUP
    slot_count = GROUP // SEQ_SHORT + 1
    key_tier, key_extra, key_full, key_short = jax.random.split(jax.random.fold_in(key, 11), 4)
    tier_draw = jax.random.randint(key_tier, (group_count, slot_count), 0, 8)
    multiple = jnp.where(tier_draw >= 7, 4, jnp.where(tier_draw >= 5, 2, 1))
    extra_len = jax.random.randint(key_extra, (group_count, slot_count), 0, SEQ_SHORT)
    lengths = jnp.minimum(multiple * SEQ_SHORT + extra_len, GROUP)
    full_group = jax.random.randint(key_full, (), 0, group_count)
    short_group = (full_group + 1 + jax.random.randint(key_short, (), 0, group_count - 1)) % group_count
    group_index = jnp.arange(group_count)[:, None]
    first_slot = jnp.arange(slot_count)[None, :] == 0
    lengths = jnp.where((group_index == full_group) & first_slot, GROUP, lengths)
    lengths = jnp.where((group_index == short_group) & first_slot, GROUP - SEQ_SHORT // 2, lengths)
    doc_ends = jnp.cumsum(lengths, axis=1)
    doc_fits = doc_ends <= GROUP
    live_counts = jnp.max(jnp.where(doc_fits, doc_ends, 0), axis=1)
    places = jnp.arange(GROUP)
    doc_ids = jnp.sum(((doc_ends[:, None, :] <= places[None, :, None]) & doc_fits[:, None, :]).astype(jnp.int32), axis=2)
    doc_ids = jnp.where(places[None, :] < live_counts[:, None], doc_ids, GROUP)
    return (doc_ids.reshape(-1).astype(jnp.int32), live_counts.astype(jnp.int32))


def draw_seq_ids(key, part):
    return packing(key)[0]


def draw_counts(key, part):
    return packing(key)[1]


def level_of(own_key, shape, pieces, low, largest):
    def one(dim, blocks):
        steps = jax.random.uniform(jax.random.fold_in(jax.random.fold_in(own_key, 6), dim), (blocks,), jnp.float32, low / len(pieces), largest / len(pieces))
        return jnp.repeat(jnp.exp(steps), shape[dim] // blocks).reshape((-1,) + (1,) * (len(shape) - dim - 1))

    gain = one(*pieces[0])
    for cut in pieces[1:]:
        gain = gain * one(*cut)
    return gain


def scatter_about(rng, shape, deviation, reach, pieces=(), kind=jnp.bfloat16):
    array = deviation * jax.random.normal(rng, shape, jnp.float32)
    if pieces:
        array = array * level_of(rng, shape, pieces, -0.22, 0.18)
    return jnp.clip(array, -reach, reach).astype(kind)


def setup_inputs(seed: int = 0) -> dict:
    keys = jax.random.split(jax.random.key(seed), 17)
    tokens = scatter_about(keys[0], (TOKENS, D), 1.0, 6.0, ((0, 32),))
    w_query = scatter_about(keys[1], (D, HEADS * HEAD_DIM), D ** -0.5, 0.1875, ((1, 4),))
    w_key = scatter_about(keys[2], (D, HEADS * HEAD_DIM), D ** -0.5, 0.1875, ((1, 4),))
    w_value = scatter_about(keys[3], (D, HEADS * HEAD_DIM), D ** -0.5, 0.1875, ((1, 4),))
    w_out = scatter_about(keys[4], (HEADS * HEAD_DIM, D), (HEADS * HEAD_DIM // 4) ** -0.5, 0.375, ((0, 4),))
    s_qk = jnp.clip(jnp.exp(math.log(1.7) - 0.53062828 * jax.random.uniform(keys[5], (HEADS * HEAD_DIM,), jnp.float32) ** level_of(keys[5], (HEADS * HEAD_DIM,), ((0, 4),), -0.2, 0.2)), 1.0, 1.7)
    alpha_attn = jnp.clip(jax.random.uniform(keys[6], (D,), jnp.float32, 0.15, 0.6), 0.15, 0.6)
    w_gate = scatter_about(keys[7], (D, FF), D ** -0.5, 0.1875, ((1, 32),))
    w_up = scatter_about(keys[8], (D, FF), D ** -0.5, 0.1875, ((1, 32),))
    w_down = scatter_about(keys[9], (D, FF), FF ** -0.5, 0.09375, ((1, 32),))
    s_gate = jnp.clip(jnp.exp(math.log(1.4) - 0.6931472 * jax.random.uniform(keys[10], (FF,), jnp.float32) ** level_of(keys[10], (FF,), ((0, 32),), -0.2, 0.2)), 0.7, 1.4)
    s_up = jnp.clip(jnp.exp(math.log(1.4) - 0.6931472 * jax.random.uniform(keys[11], (FF,), jnp.float32) ** level_of(keys[11], (FF,), ((0, 32),), -0.2, 0.2)), 0.7, 1.4)
    alpha_mlp = jnp.clip(jax.random.uniform(keys[12], (D,), jnp.float32, 0.15, 0.6), 0.15, 0.6)
    seq_ids = draw_seq_ids(jax.random.fold_in(keys[16], 71), 0)
    counts = draw_counts(jax.random.fold_in(keys[16], 71), 0)
    out_grad = scatter_about(keys[15], (TOKENS, D), 1.0, 6.0, ((0, 32),), jnp.float32)
    return {"tokens": tokens, "w_query": w_query, "w_key": w_key, "w_value": w_value, "w_out": w_out, "s_qk": s_qk, "alpha_attn": alpha_attn, "w_gate": w_gate, "w_up": w_up, "w_down": w_down, "s_gate": s_gate, "s_up": s_up, "alpha_mlp": alpha_mlp, "seq_ids": seq_ids, "counts": counts, "out_grad": out_grad}


epsilon = 1e-06
highest = lax.Precision.HIGHEST
masked_score = -1e+30

@jax.custom_vjp
def low(v):
    return lax.optimization_barrier(v.astype(jnp.bfloat16)).astype(jnp.float32)

@jax.custom_vjp
def low_back(v):
    return v

def low_keep(v):
    return (low(v), None)

def low_pass(kept, grad):
    return (grad,)

def back_keep(v):
    return (v, None)

def back_low(kept, grad):
    return (low(grad),)
low.defvjp(low_keep, low_pass)
low_back.defvjp(back_keep, back_low)

def unit_rms(values):
    return values * lax.rsqrt(lax.optimization_barrier(jnp.mean(values * values, axis=-1, keepdims=True)) + epsilon)

def matmul(left, right):
    return jnp.dot(left, right, precision=highest, preferred_element_type=jnp.float32)

def rotary_tables(seq_ids):
    blocked = seq_ids.reshape(-1, GROUP)
    row_index = jnp.arange(GROUP, dtype=jnp.int32)
    changed = jnp.concatenate([jnp.ones((blocked.shape[0], 1), dtype=bool), blocked[:, 1:] != blocked[:, :-1]], axis=1)
    starts = lax.cummax(jnp.where(changed, row_index[None, :], 0), axis=1)
    places = (row_index[None, :] - starts).astype(jnp.float32)
    frequency = 10000.0 ** (-(2.0 * jnp.arange(HEAD_DIM // 2, dtype=jnp.float32)) / HEAD_DIM)
    angles = places.reshape(-1)[:, None] * frequency[None, :]
    return (jnp.cos(angles), jnp.sin(angles))

def rotate(values, cos_tab, sine_tab):
    half_dim = values.shape[-1] // 2
    first_half = values[..., :half_dim]
    second_half = values[..., half_dim:]
    cos_b = cos_tab[:, None, :]
    sine_b = sine_tab[:, None, :]
    return jnp.concatenate([first_half * cos_b - second_half * sine_b, second_half * cos_b + first_half * sine_b], axis=-1)

def attend_group(operands):
    queries, keys_in, values_in, group_ids = operands
    row_index = jnp.arange(GROUP, dtype=jnp.int32)
    allowed = (group_ids[:, None] == group_ids[None, :]) & (row_index[:, None] >= row_index[None, :]) & ((group_ids[:, None] < GROUP) | (row_index[:, None] == row_index[None, :]))
    score_scale = HEAD_DIM ** (-0.5)

    def one_head(head_ops):
        query_h, key_h, value_h = head_ops
        scores = low_back(matmul(query_h, key_h.T) * score_scale)
        scores = jnp.where(allowed, scores, masked_score)
        attn_probs = jax.nn.softmax(scores, axis=-1)
        return matmul(low(attn_probs), value_h)
    result = lax.map(jax.checkpoint(one_head), (queries.transpose(1, 0, 2), keys_in.transpose(1, 0, 2), values_in.transpose(1, 0, 2)))
    return result.transpose(1, 0, 2)

def forward(tokens, w_query, w_key, w_value, w_out, s_qk, alpha_attn, w_gate, w_up, w_down, s_gate, s_up, alpha_mlp, cos_tab, sine_tab, seq_ids):
    token_count = tokens.shape[0]
    head_shape = (token_count, HEADS, HEAD_DIM)
    qk_scale = s_qk.reshape(HEADS, HEAD_DIM)
    query_raw = low_back(matmul(tokens, w_query)).reshape(head_shape)
    key_raw = low_back(matmul(tokens, w_key)).reshape(head_shape)
    value_n = low(low_back(matmul(tokens, w_value))).reshape(head_shape)
    query_n = low(unit_rms(rotate(query_raw, cos_tab, sine_tab)) * qk_scale)
    key_n = low(unit_rms(rotate(key_raw, cos_tab, sine_tab)) * qk_scale)
    grouped = (-1, GROUP, HEADS, HEAD_DIM)
    attended = lax.map(attend_group, (query_n.reshape(grouped), key_n.reshape(grouped), value_n.reshape(grouped), seq_ids.reshape(-1, GROUP)))
    attended = low(low_back(attended.reshape(token_count, HEADS * HEAD_DIM)))
    attn_mix = low_back(matmul(attended, w_out))
    after_attn = unit_rms(tokens + alpha_attn * (unit_rms(attn_mix) - tokens))
    mid_low = low(after_attn)
    up_raw = low_back(matmul(mid_low, w_up))
    gate_raw = low_back(matmul(mid_low, w_gate))
    inner_act = low(up_raw * s_up * jax.nn.silu(gate_raw * s_gate))
    mlp_out = low_back(matmul(inner_act, w_down.T))
    return unit_rms(after_attn + alpha_mlp * (unit_rms(mlp_out) - after_attn))

def reference(tokens, w_query, w_key, w_value, w_out, s_qk, alpha_attn, w_gate, w_up, w_down, s_gate, s_up, alpha_mlp, seq_ids, counts, out_grad):
    cos_tab, sine_tab = rotary_tables(seq_ids)
    live_rows = (jnp.arange(GROUP, dtype=jnp.int32)[None, :] < counts[:, None]).reshape(-1).astype(jnp.float32)
    params = (tokens.astype(jnp.float32), w_query.astype(jnp.float32), w_key.astype(jnp.float32), w_value.astype(jnp.float32), w_out.astype(jnp.float32), s_qk, alpha_attn, w_gate.astype(jnp.float32), w_up.astype(jnp.float32), w_down.astype(jnp.float32), s_gate, s_up, alpha_mlp)

    def wrapped(*inputs_all):
        return forward(*inputs_all, cos_tab, sine_tab, seq_ids)
    result, pullback = jax.vjp(wrapped, *params)
    gradients = pullback(out_grad.astype(jnp.float32) * live_rows[:, None])
    squares_sum = jnp.float32(0.0)
    for weight_grad in gradients[1:]:
        squares_sum = squares_sum + jnp.sum(weight_grad * weight_grad)
    grad_norm = jnp.sqrt(squares_sum)
    mean_alpha = jnp.mean(jnp.concatenate([alpha_attn, alpha_mlp]))
    return (result.astype(jnp.bfloat16), gradients[0], gradients[1], gradients[2], gradients[3], gradients[4], gradients[5], gradients[6], gradients[7], gradients[8], gradients[9], gradients[10], gradients[11], gradients[12], grad_norm, mean_alpha)
```

```python
import jax
import jax.numpy as jnp
from jax import lax
from jax.sharding import PartitionSpec as P

HEAD_DIM = 64


epsilon = 1e-06
masked_score = -1e30
row_contract = (((1,), (1,)), ((), ()))
col_contract = (((0,), (0,)), ((), ()))


def unit_rms(values):
    return values * lax.rsqrt(jnp.mean(values * values, axis=-1, keepdims=True) + epsilon)


def rms_back(values, grad_in):
    factor = lax.rsqrt(jnp.mean(values * values, axis=-1, keepdims=True) + epsilon)
    normed = values * factor
    return factor * (grad_in - normed * jnp.mean(grad_in * normed, axis=-1, keepdims=True))


def rotary_tables(seq_ids):
    row_index = jnp.arange(seq_ids.shape[0], dtype=jnp.int32)
    changed = jnp.concatenate([jnp.ones((1,), dtype=bool), seq_ids[1:] != seq_ids[:-1]])
    starts = lax.cummax(jnp.where(changed, row_index, 0), axis=0)
    places = (row_index - starts).astype(jnp.float32)
    frequency = 10000.0 ** (-(2.0 * jnp.arange(HEAD_DIM // 2, dtype=jnp.float32)) / HEAD_DIM)
    angles = places[:, None] * frequency[None, :]
    return (jnp.cos(angles), jnp.sin(angles))


def rotate(values, cos_tab, sine_tab):
    half_dim = values.shape[-1] // 2
    first_half = values[..., :half_dim]
    second_half = values[..., half_dim:]
    cos_b = cos_tab[:, None, :]
    sine_b = sine_tab[:, None, :]
    return jnp.concatenate(
        [first_half * cos_b - second_half * sine_b, second_half * cos_b + first_half * sine_b],
        axis=-1,
    )


def block_allowed(seq_ids, q_first, k_first, block_rows):
    pad_id = seq_ids.shape[0]
    query_ids = lax.dynamic_slice_in_dim(seq_ids, q_first, block_rows, 0)
    key_ids = lax.dynamic_slice_in_dim(seq_ids, k_first, block_rows, 0)
    query_rows = q_first + jnp.arange(block_rows, dtype=jnp.int32)
    key_rows = k_first + jnp.arange(block_rows, dtype=jnp.int32)
    same_doc = query_ids[:, None] == key_ids[None, :]
    causal = query_rows[:, None] >= key_rows[None, :]
    diagonal = query_rows[:, None] == key_rows[None, :]
    return (same_doc & causal & ((query_ids[:, None] < pad_id) | diagonal))[None, :, :]


def block_live(seq_ids, q_block, k_block, block_rows):
    pad_id = seq_ids.shape[0]
    query_low = lax.dynamic_index_in_dim(seq_ids, q_block * block_rows, 0, keepdims=False)
    key_high = lax.dynamic_index_in_dim(
        seq_ids, k_block * block_rows + block_rows - 1, 0, keepdims=False
    )
    return (q_block == k_block) | (key_high == query_low) & (query_low < pad_id)


def block_scores(query_n, key_n, seq_ids, q_block, k_block, block_rows):
    q_first = q_block * block_rows
    k_first = k_block * block_rows
    query_part = lax.dynamic_slice_in_dim(query_n, q_first, block_rows, 0)
    key_part = lax.dynamic_slice_in_dim(key_n, k_first, block_rows, 0)
    score_scale = query_n.shape[2] ** (-0.5)
    scores = (
        jnp.einsum("qhd,khd->hqk", query_part, key_part, preferred_element_type=jnp.float32)
        * score_scale
    )
    return (scores, block_allowed(seq_ids, q_first, k_first, block_rows))


def attention_forward(query_n, key_n, value_n, seq_ids, block_rows):
    group_rows, local_heads, head_dim = query_n.shape
    block_count = group_rows // block_rows

    def one_query(q_block):

        def stats_step(k_block, carried):

            def stats_update(state_in):
                run_max, run_sum = state_in
                scores, allowed = block_scores(
                    query_n, key_n, seq_ids, q_block, k_block, block_rows
                )
                new_max = jnp.maximum(
                    run_max, jnp.max(jnp.where(allowed, scores, masked_score), axis=-1)
                )
                shifted = jnp.exp(jnp.where(allowed, scores - new_max[:, :, None], masked_score))
                return (new_max, run_sum * jnp.exp(run_max - new_max) + jnp.sum(shifted, axis=-1))

            return lax.cond(
                block_live(seq_ids, q_block, k_block, block_rows),
                stats_update,
                lambda kept_state: kept_state,
                carried,
            )

        initial = (
            jnp.full((local_heads, block_rows), masked_score, jnp.float32),
            jnp.zeros((local_heads, block_rows), jnp.float32),
        )
        run_max, run_sum = lax.fori_loop(0, q_block + 1, stats_step, initial)
        log_norm = run_max + jnp.log(run_sum)

        def value_step(k_block, accum_in):

            def value_update(accum):
                scores, allowed = block_scores(
                    query_n, key_n, seq_ids, q_block, k_block, block_rows
                )
                attn_probs = jnp.exp(
                    jnp.where(allowed, scores - log_norm[:, :, None], masked_score)
                ).astype(jnp.bfloat16)
                value_part = lax.dynamic_slice_in_dim(value_n, k_block * block_rows, block_rows, 0)
                return accum + jnp.einsum(
                    "hqk,khd->qhd", attn_probs, value_part, preferred_element_type=jnp.float32
                )

            return lax.cond(
                block_live(seq_ids, q_block, k_block, block_rows),
                value_update,
                lambda kept_state: kept_state,
                accum_in,
            )

        attn_out = lax.fori_loop(
            0, q_block + 1, value_step, jnp.zeros((block_rows, local_heads, head_dim), jnp.float32)
        )
        return (attn_out, log_norm)

    outputs, log_norms = lax.map(one_query, jnp.arange(block_count, dtype=jnp.int32))
    return (outputs.reshape(group_rows, local_heads, head_dim), log_norms)


def attention_backward(query_n, key_n, value_n, seq_ids, log_norms, grad_out, attn_out, block_rows):
    group_rows, local_heads, head_dim = query_n.shape
    block_count = group_rows // block_rows
    score_scale = head_dim ** (-0.5)
    row_delta = jnp.sum(grad_out.astype(jnp.float32) * attn_out, axis=-1)

    def query_step(q_block, carried):
        grad_query, grad_key, grad_value = carried
        q_first = q_block * block_rows
        query_part = lax.dynamic_slice_in_dim(query_n, q_first, block_rows, 0)
        grad_part = lax.dynamic_slice_in_dim(grad_out, q_first, block_rows, 0)
        delta_part = lax.dynamic_slice_in_dim(row_delta, q_first, block_rows, 0).T
        log_norm = log_norms[q_block]

        def key_step(k_block, inner_state):

            def key_update(state_in):
                q_grad, k_grad, v_grad = state_in
                k_first = k_block * block_rows
                scores, allowed = block_scores(
                    query_n, key_n, seq_ids, q_block, k_block, block_rows
                )
                attn_probs = jnp.exp(
                    jnp.where(allowed, scores - log_norm[:, :, None], masked_score)
                )
                key_part = lax.dynamic_slice_in_dim(key_n, k_first, block_rows, 0)
                value_part = lax.dynamic_slice_in_dim(value_n, k_first, block_rows, 0)
                grad_probs = jnp.einsum(
                    "qhd,khd->hqk", grad_part, value_part, preferred_element_type=jnp.float32
                )
                grad_scores = (attn_probs * (grad_probs - delta_part[:, :, None])).astype(
                    jnp.bfloat16
                )
                q_grad = (
                    q_grad
                    + jnp.einsum(
                        "hqk,khd->qhd", grad_scores, key_part, preferred_element_type=jnp.float32
                    )
                    * score_scale
                )
                key_add = (
                    jnp.einsum(
                        "hqk,qhd->khd", grad_scores, query_part, preferred_element_type=jnp.float32
                    )
                    * score_scale
                )
                value_add = jnp.einsum(
                    "hqk,qhd->khd",
                    attn_probs.astype(jnp.bfloat16),
                    grad_part,
                    preferred_element_type=jnp.float32,
                )
                k_grad = lax.dynamic_update_slice_in_dim(
                    k_grad,
                    lax.dynamic_slice_in_dim(k_grad, k_first, block_rows, 0) + key_add,
                    k_first,
                    0,
                )
                v_grad = lax.dynamic_update_slice_in_dim(
                    v_grad,
                    lax.dynamic_slice_in_dim(v_grad, k_first, block_rows, 0) + value_add,
                    k_first,
                    0,
                )
                return (q_grad, k_grad, v_grad)

            return lax.cond(
                block_live(seq_ids, q_block, k_block, block_rows),
                key_update,
                lambda kept_state: kept_state,
                inner_state,
            )

        start_state = (
            jnp.zeros((block_rows, local_heads, head_dim), jnp.float32),
            grad_key,
            grad_value,
        )
        q_grad, grad_key, grad_value = lax.fori_loop(0, q_block + 1, key_step, start_state)
        grad_query = lax.dynamic_update_slice_in_dim(grad_query, q_grad, q_first, 0)
        return (grad_query, grad_key, grad_value)

    zeros_full = jnp.zeros(query_n.shape, jnp.float32)
    return lax.fori_loop(0, block_count, query_step, (zeros_full, zeros_full, zeros_full))


def bits_of(size):
    return [1 << k for k in range(size.bit_length() - 1)]


def flip(values, axis, bit):
    size = lax.axis_size(axis)
    return lax.ppermute(values, axis, [(k, k ^ bit) for k in range(size)])


def gather_parts(own, axis):
    parts = {0: own}
    for bit in reversed(bits_of(lax.axis_size(axis))):
        for slot in list(parts):
            parts[slot ^ bit] = flip(parts[slot], axis, bit)
    return parts


def scatter_parts(parts, axis):
    for bit in bits_of(lax.axis_size(axis)):
        kept = {}
        for slot in parts:
            if not slot & bit:
                kept[slot] = parts[slot] + flip(
                    parts[slot | bit].astype(jnp.bfloat16), axis, bit
                ).astype(jnp.float32)
        parts = kept
    return parts[0]


def butterfly(values, axis):
    for bit in bits_of(lax.axis_size(axis)):
        values = values + flip(values, axis, bit)
    return values


def gather_columns(own):
    whole = own
    for bit in reversed(bits_of(lax.axis_size("dp"))):
        whole = jnp.concatenate([whole, flip(whole, "dp", bit)], axis=1)
    return whole


def scatter_columns(low_half, high_half, kind=jnp.bfloat16):
    for bit in bits_of(lax.axis_size("dp")):
        whole = low_half + flip(high_half.astype(kind), "dp", bit).astype(jnp.float32)
        middle = whole.shape[1] // 2
        low_half, high_half = whole[:, :middle], whole[:, middle:]
    return whole


def scatter_rows(whole):
    rank = lax.axis_index("dp")
    for bit in bits_of(lax.axis_size("dp")):
        middle = whole.shape[0] // 2
        upper = (rank & bit) // bit
        sent = lax.dynamic_slice_in_dim(whole, (1 - upper) * middle, middle, 0)
        kept = lax.dynamic_slice_in_dim(whole, upper * middle, middle, 0)
        whole = kept + flip(sent.astype(jnp.bfloat16), "dp", bit).astype(jnp.float32)
    return whole


def gather_rows(own):
    rank = lax.axis_index("dp")
    for bit in reversed(bits_of(lax.axis_size("dp"))):
        other = flip(own, "dp", bit)
        own = jnp.where(
            (rank & bit) > 0,
            jnp.concatenate([other, own], axis=0),
            jnp.concatenate([own, other], axis=0),
        )
    return own


def swap_blocks(values, count):
    rank = lax.axis_index("head")
    rows = values.shape[0] // count
    return jnp.concatenate(
        [lax.dynamic_slice_in_dim(values, (rank ^ k) * rows, rows, 0) for k in range(count)],
        axis=0,
    )


def local(
    tokens,
    w_query,
    w_key,
    w_value,
    w_out,
    s_qk,
    alpha_attn,
    w_gate,
    w_up,
    w_down,
    s_gate,
    s_up,
    alpha_mlp,
    seq_ids,
    counts,
    out_grad,
):
    head_count = lax.axis_size("head")
    head_rank = lax.axis_index("head")
    own_rows, model_width = tokens.shape
    group_rows = own_rows * head_count
    head_cols = w_query.shape[1]
    local_heads = head_cols // HEAD_DIM
    block_rows = min(512, group_rows)
    head_shape = (group_rows, local_heads, HEAD_DIM)
    half_slots = [list(range(head_count // 2)), list(range(head_count // 2, head_count))]

    def gather_halves(own):
        parts = gather_parts(own, "head")
        return [jnp.concatenate([parts[k] for k in slots], axis=0) for slots in half_slots]

    def scatter_halves(halves):
        parts = {}
        for values, slots in zip(halves, half_slots):
            for place, slot in enumerate(slots):
                parts[slot] = values[place * own_rows : (place + 1) * own_rows]
        return scatter_parts(parts, "head")

    group_tokens = swap_blocks(jnp.concatenate(gather_halves(tokens), axis=0), head_count)
    gate_w = gather_columns(w_gate)
    up_w = gather_columns(w_up)
    scales = gather_columns(jnp.stack([s_gate, s_up]))
    down_w = gather_columns(w_down)
    gate_scale, up_scale = scales[0:1], scales[1:2]
    projections = jnp.concatenate([w_query, w_key, w_value], axis=1)
    projected = jnp.dot(group_tokens, projections, preferred_element_type=jnp.float32)
    cos_tab, sine_tab = rotary_tables(seq_ids)
    qk_scale = s_qk.reshape(local_heads, HEAD_DIM)
    query_rot = rotate(projected[:, :head_cols].reshape(head_shape), cos_tab, sine_tab)
    key_rot = rotate(projected[:, head_cols : 2 * head_cols].reshape(head_shape), cos_tab, sine_tab)
    query_unit = unit_rms(query_rot)
    key_unit = unit_rms(key_rot)
    query_n = (query_unit * qk_scale).astype(jnp.bfloat16)
    key_n = (key_unit * qk_scale).astype(jnp.bfloat16)
    value_n = projected[:, 2 * head_cols :].reshape(head_shape).astype(jnp.bfloat16)
    attended, log_norms = attention_forward(query_n, key_n, value_n, seq_ids, block_rows)
    attended_b = swap_blocks(
        attended.reshape(group_rows, head_cols).astype(jnp.bfloat16), head_count
    )
    half_rows = group_rows // 2
    attn_mix = scatter_halves(
        [
            jnp.dot(attended_b[k * half_rows : (k + 1) * half_rows], w_out, preferred_element_type=jnp.float32)
            for k in range(2)
        ]
    )
    residual = tokens.astype(jnp.float32)
    attn_unit = unit_rms(attn_mix)
    first_sum = residual + alpha_attn * (attn_unit - residual)
    after_attn = unit_rms(first_sum)
    mids = gather_halves(after_attn.astype(jnp.bfloat16))

    def forward_units(mid_rows):
        gate_raw = jnp.dot(mid_rows, gate_w, preferred_element_type=jnp.float32)
        up_raw = jnp.dot(mid_rows, up_w, preferred_element_type=jnp.float32)
        inner = (up_raw * up_scale * jax.nn.silu(gate_raw * gate_scale)).astype(jnp.bfloat16)
        part = lax.dot_general(inner, down_w, row_contract, preferred_element_type=jnp.float32)
        return gate_raw, up_raw, inner, part

    kept = [forward_units(rows) for rows in mids]
    mlp_out = scatter_halves([k[3] for k in kept])
    mlp_unit = unit_rms(mlp_out)
    second_sum = after_attn + alpha_mlp * (mlp_unit - after_attn)
    output = unit_rms(second_sum)
    row_ids = head_rank * own_rows + jnp.arange(own_rows, dtype=jnp.int32)
    live_rows = (row_ids < counts[0]).astype(jnp.float32)
    grad_second = rms_back(second_sum, out_grad * live_rows[:, None])
    alpha_mlp_grad = jnp.sum(grad_second * (mlp_unit - after_attn), axis=0)
    grad_mlps = gather_halves(rms_back(mlp_out, grad_second * alpha_mlp).astype(jnp.bfloat16))

    def backward_units(grad_rows, gate_raw, up_raw):
        gate_pre = gate_raw * gate_scale
        up_pre = up_raw * up_scale
        gate_act = jax.nn.silu(gate_pre)
        gate_sig = jax.nn.sigmoid(gate_pre)
        grad_inner = jnp.dot(grad_rows, down_w, preferred_element_type=jnp.float32)
        grad_up_pre = grad_inner * gate_act
        grad_gate_pre = grad_inner * up_pre * gate_sig * (1.0 + gate_pre * (1.0 - gate_sig))
        scale_terms = jnp.stack(
            [jnp.sum(grad_gate_pre * gate_raw, axis=0), jnp.sum(grad_up_pre * up_raw, axis=0)]
        )
        gate_back = (grad_gate_pre * gate_scale).astype(jnp.bfloat16)
        up_back = (grad_up_pre * up_scale).astype(jnp.bfloat16)
        grad_mid = lax.dot_general(
            gate_back, gate_w, row_contract, preferred_element_type=jnp.float32
        ) + lax.dot_general(up_back, up_w, row_contract, preferred_element_type=jnp.float32)
        return gate_back, up_back, scale_terms, grad_mid

    backs = [backward_units(rows, k[0], k[1]) for rows, k in zip(grad_mlps, kept)]
    grad_mid = scatter_halves([b[3] for b in backs])

    unit_half = gate_w.shape[1] // 2

    def unit_grads(lefts, rights):
        left = jnp.concatenate(lefts, axis=0)
        right = jnp.concatenate(rights, axis=0)
        return scatter_columns(
            *[
                lax.dot_general(
                    left,
                    right[:, k * unit_half : (k + 1) * unit_half],
                    col_contract,
                    preferred_element_type=jnp.float32,
                )
                for k in range(2)
            ]
        )

    down_grad = unit_grads(grad_mlps, [k[2] for k in kept])
    gate_grad = unit_grads(mids, [b[0] for b in backs])
    up_grad = unit_grads(mids, [b[1] for b in backs])
    scale_terms = backs[0][2] + backs[1][2]
    scale_grads = scatter_columns(
        scale_terms[:, :unit_half], scale_terms[:, unit_half:], jnp.float32
    )

    grad_after = grad_second * (1.0 - alpha_mlp) + grad_mid
    grad_first = rms_back(first_sum, grad_after)
    alpha_attn_grad = jnp.sum(grad_first * (attn_unit - residual), axis=0)
    grad_mix = rms_back(attn_mix, grad_first * alpha_attn).astype(jnp.bfloat16)
    grad_mix_group = jnp.concatenate(gather_halves(grad_mix), axis=0)
    out_chunk = scatter_rows(
        lax.dot_general(
            attended_b, grad_mix_group, col_contract, preferred_element_type=jnp.float32
        )
    )
    grad_attended = lax.dot_general(
        grad_mix_group, w_out, row_contract, preferred_element_type=jnp.float32
    )
    grad_attended = swap_blocks(grad_attended.astype(jnp.bfloat16), head_count).reshape(head_shape)
    grad_qn, grad_kn, grad_vn = attention_backward(
        query_n, key_n, value_n, seq_ids, log_norms, grad_attended, attended, block_rows
    )
    qk_grad = jnp.sum(grad_qn * query_unit + grad_kn * key_unit, axis=0).reshape(-1)
    grad_q_raw = rotate(rms_back(query_rot, grad_qn * qk_scale), cos_tab, -sine_tab)
    grad_k_raw = rotate(rms_back(key_rot, grad_kn * qk_scale), cos_tab, -sine_tab)
    grad_projected = jnp.concatenate(
        [
            grad_q_raw.reshape(group_rows, head_cols),
            grad_k_raw.reshape(group_rows, head_cols),
            grad_vn.reshape(group_rows, head_cols),
        ],
        axis=1,
    ).astype(jnp.bfloat16)
    proj_chunk = scatter_rows(
        lax.dot_general(
            group_tokens, grad_projected, col_contract, preferred_element_type=jnp.float32
        )
    )
    relative = swap_blocks(grad_projected, head_count)
    grad_input = scatter_halves(
        [
            lax.dot_general(
                relative[k * half_rows : (k + 1) * half_rows],
                projections,
                row_contract,
                preferred_element_type=jnp.float32,
            )
            for k in range(2)
        ]
    ) + grad_first * (1.0 - alpha_attn)
    proj_sum = gather_rows(proj_chunk.astype(jnp.bfloat16)).astype(jnp.float32)
    out_sum = gather_rows(out_chunk.astype(jnp.bfloat16)).astype(jnp.float32)
    qk_sum = butterfly(qk_grad, "dp")
    alpha_sum = butterfly(
        butterfly(jnp.stack([alpha_attn_grad, alpha_mlp_grad]), "head"), "dp"
    )
    squares = (
        sum(jnp.sum(g * g) for g in (proj_chunk, out_chunk, down_grad, gate_grad, up_grad, scale_grads))
        + jnp.sum(qk_sum * qk_sum) / lax.axis_size("dp")
    )
    square_sum = butterfly(butterfly(jnp.full((8, 128), squares), "dp"), "head")[0, 0]
    grad_norm = jnp.sqrt(square_sum + jnp.sum(alpha_sum * alpha_sum))
    mean_alpha = jnp.mean(jnp.concatenate([alpha_attn, alpha_mlp]))
    return (
        output.astype(jnp.bfloat16),
        grad_input,
        proj_sum[:, :head_cols],
        proj_sum[:, head_cols : 2 * head_cols],
        proj_sum[:, 2 * head_cols :],
        out_sum,
        qk_sum,
        alpha_sum[0],
        gate_grad,
        up_grad,
        down_grad,
        scale_grads[0],
        scale_grads[1],
        alpha_sum[1],
        grad_norm,
        mean_alpha,
    )


def solution(mesh):
    in_specs = (
        P(("dp", "head"), None),
        P(None, "head"),
        P(None, "head"),
        P(None, "head"),
        P("head", None),
        P("head"),
        P(),
        P(None, ("dp", "head")),
        P(None, ("dp", "head")),
        P(None, ("dp", "head")),
        P(("dp", "head")),
        P(("dp", "head")),
        P(),
        P("dp"),
        P("dp"),
        P(("dp", "head"), None),
    )
    out_specs = (
        P(("dp", "head"), None),
        P(("dp", "head"), None),
        P(None, "head"),
        P(None, "head"),
        P(None, "head"),
        P("head", None),
        P("head"),
        P(),
        P(None, ("dp", "head")),
        P(None, ("dp", "head")),
        P(None, ("dp", "head")),
        P(("dp", "head")),
        P(("dp", "head")),
        P(),
        P(),
        P(),
    )
    return jax.shard_map(local, mesh=mesh, in_specs=in_specs, out_specs=out_specs, check_vma=False)
```

```python
import jax
import jax.numpy as jnp
from jax import lax
from jax.experimental import pallas as pl
from jax.experimental.pallas import tpu as pltpu
from jax.sharding import PartitionSpec as P

HEAD_DIM = 64
LANES = 128


epsilon = 1e-06
row_contract = (((1,), (1,)), ((), ()))
col_contract = (((0,), (0,)), ((), ()))


def unit_rms(values):
    return values * lax.rsqrt(jnp.mean(values * values, axis=-1, keepdims=True) + epsilon)


def rms_back(values, grad_in):
    factor = lax.rsqrt(jnp.mean(values * values, axis=-1, keepdims=True) + epsilon)
    normed = values * factor
    return factor * (grad_in - normed * jnp.mean(grad_in * normed, axis=-1, keepdims=True))


def segment_mean(values, spread):
    upper = values.astype(jnp.bfloat16)
    lower = (values - upper.astype(jnp.float32)).astype(jnp.bfloat16)
    return jnp.dot(upper, spread, preferred_element_type=jnp.float32) + jnp.dot(
        lower, spread, preferred_element_type=jnp.float32
    )


def swap_halves(values):
    lane = lax.broadcasted_iota(jnp.int32, values.shape, 1)
    return jnp.where(
        lane % HEAD_DIM < HEAD_DIM // 2,
        pltpu.roll(values, LANES - HEAD_DIM // 2, 1),
        pltpu.roll(values, HEAD_DIM // 2, 1),
    )


def spread_matrix():
    row = lax.broadcasted_iota(jnp.int32, (LANES, LANES), 0) // HEAD_DIM
    col = lax.broadcasted_iota(jnp.int32, (LANES, LANES), 1) // HEAD_DIM
    return jnp.where(row == col, 1.0 / HEAD_DIM, 0.0).astype(jnp.bfloat16)


def turned_unit(raw, cos_b, sine_b, spread):
    turned = raw * cos_b + swap_halves(raw) * sine_b
    factor = lax.rsqrt(segment_mean(turned * turned, spread) + epsilon)
    return turned * factor, factor


def head_masks(shape):
    lane = lax.broadcasted_iota(jnp.int32, shape, 1)
    return [lane // HEAD_DIM == k for k in range(LANES // HEAD_DIM)]


def attend_kernel(rank_ref, q_ref, k_ref, v_ref, cos_ref, sine_ref, scale_ref, idc_ref, idr_ref,
                  out_ref, log_ref, q_heads, k_all, v_wide, acc):
    blocks, _, rows = idr_ref.shape
    rank = rank_ref[0]
    spread = spread_matrix()
    masks = head_masks((rows, LANES))
    scale = scale_ref[...]

    def prepare(block, carry):
        at = pl.ds(pl.multiple_of(block * rows, rows), rows)
        cos_b, sine_b = cos_ref[at, :], sine_ref[at, :]
        q_unit, _ = turned_unit(q_ref[at, :], cos_b, sine_b, spread)
        k_unit, _ = turned_unit(k_ref[at, :], cos_b, sine_b, spread)
        q_norm = q_unit * scale * HEAD_DIM ** (-0.5)
        for head, mask in enumerate(masks):
            q_heads[head, at, :] = jnp.where(mask, q_norm, 0.0).astype(jnp.bfloat16)
        k_all[at, :] = (k_unit * scale).astype(jnp.bfloat16)
        v_wide[at, :LANES] = v_ref[at, :].astype(jnp.bfloat16)
        v_wide[at, LANES:] = jnp.ones((rows, LANES), jnp.bfloat16)
        return carry

    lax.fori_loop(0, blocks, prepare, 0)
    ones_rows = jnp.ones((8, rows), jnp.bfloat16)

    def query_step(q_block, carry):
        q_place = q_block ^ rank
        q_at = pl.ds(pl.multiple_of(q_place * rows, rows), rows)
        id_col = idc_ref[q_at, :]

        def one_block(k_place, sums, first, extra):
            k_at = pl.ds(pl.multiple_of(k_place * rows, rows), rows)
            keys = k_all[k_at, :]
            values = v_wide[k_at, :]
            allowed = id_col == idr_ref[k_place]
            if extra is not None:
                allowed = allowed & extra
            new_sums = []
            for head in range(len(masks)):
                scores = lax.dot_general(
                    q_heads[head, q_at, :], keys, row_contract, preferred_element_type=jnp.float32
                )
                probs = jnp.where(allowed, jnp.exp(scores), 0.0).astype(jnp.bfloat16)
                part = jnp.dot(probs, values, preferred_element_type=jnp.float32)
                acc[head] = part if first else acc[head] + part
                row_sum = lax.dot_general(
                    ones_rows, probs, row_contract, preferred_element_type=jnp.float32
                )
                new_sums.append(row_sum if first else sums[head] + row_sum)
            return tuple(new_sums)

        diagonal = lax.broadcasted_iota(jnp.int32, (rows, rows), 0) >= lax.broadcasted_iota(
            jnp.int32, (rows, rows), 1
        )
        sums = one_block(q_place, None, True, diagonal)
        sums = lax.fori_loop(
            0, q_block, lambda k_block, s: one_block(k_block ^ rank, s, False, None), sums
        )
        result = acc[0][:, :LANES] / acc[0][:, LANES:]
        for head in range(1, len(masks)):
            result = jnp.where(masks[head], acc[head][:, :LANES] / acc[head][:, LANES:], result)
        out_ref[q_at, :] = result.astype(jnp.bfloat16)
        for head in range(len(masks)):
            log_ref[head, q_place] = jnp.log(sums[head][:1])
        return carry

    lax.fori_loop(0, blocks, query_step, 0)


def attend_back_kernel(rank_ref, q_ref, k_ref, v_ref, cos_ref, sine_ref, scale_ref, idc_ref, idr_ref,
                       out_ref, grad_ref, log_ref,
                       gq_ref, gk_ref, gv_ref, gs_ref,
                       q_heads, k_heads, k_all, v_all, g_heads, delta, dq):
    blocks, _, rows = idr_ref.shape
    heads = LANES // HEAD_DIM
    rank = rank_ref[0]
    spread = spread_matrix()
    masks = head_masks((rows, LANES))
    scale = scale_ref[...]
    lane8 = lax.broadcasted_iota(jnp.int32, (8, LANES), 1) // HEAD_DIM

    def prepare(block, carry):
        at = pl.ds(pl.multiple_of(block * rows, rows), rows)
        cos_b, sine_b = cos_ref[at, :], sine_ref[at, :]
        q_unit, _ = turned_unit(q_ref[at, :], cos_b, sine_b, spread)
        k_unit, _ = turned_unit(k_ref[at, :], cos_b, sine_b, spread)
        q_norm = q_unit * scale * HEAD_DIM ** (-0.5)
        k_norm = k_unit * scale
        grads = grad_ref[at, :]
        product = grads.astype(jnp.float32) * out_ref[at, :].astype(jnp.float32)
        upper = product.astype(jnp.bfloat16)
        lower = (product - upper.astype(jnp.float32)).astype(jnp.bfloat16)
        for head, mask in enumerate(masks):
            q_heads[head, at, :] = jnp.where(mask, q_norm, 0.0).astype(jnp.bfloat16)
            k_heads[head, at, :] = jnp.where(mask, k_norm, 0.0).astype(jnp.bfloat16)
            g_heads[head, at, :] = jnp.where(mask, grads, jnp.zeros_like(grads))
            pick = jnp.where(lane8 == head, 1.0, 0.0).astype(jnp.bfloat16)
            delta[head, block] = (
                lax.dot_general(pick, upper, row_contract, preferred_element_type=jnp.float32)
                + lax.dot_general(pick, lower, row_contract, preferred_element_type=jnp.float32)
            )[:1]
        k_all[at, :] = k_norm.astype(jnp.bfloat16)
        v_all[at, :] = v_ref[at, :].astype(jnp.bfloat16)
        dq[at, :] = jnp.zeros((rows, LANES), jnp.float32)
        return carry

    lax.fori_loop(0, blocks, prepare, 0)
    gs_ref[...] = jnp.zeros(gs_ref.shape, jnp.float32)

    def finish(grad, raw, at):
        cos_b, sine_b = cos_ref[at, :], sine_ref[at, :]
        unit, factor = turned_unit(raw, cos_b, sine_b, spread)
        gs_ref[...] += jnp.sum((grad * unit).reshape(rows // 8, 8, LANES), axis=0)
        grad = grad * scale
        back = factor * (grad - unit * segment_mean(grad * unit, spread))
        return (back * cos_b - swap_halves(back) * sine_b).astype(jnp.bfloat16)

    def key_step(k_block, carry):
        k_place = k_block ^ rank
        k_at = pl.ds(pl.multiple_of(k_place * rows, rows), rows)
        keys = k_all[k_at, :]
        values = v_all[k_at, :]
        id_col = idc_ref[k_at, :]

        def one_block(q_place, state, extra):
            q_at = pl.ds(pl.multiple_of(q_place * rows, rows), rows)
            allowed = id_col == idr_ref[q_place]
            if extra is not None:
                allowed = allowed & extra
            dk, dv = state
            dq_part = None
            for head in range(heads):
                queries = q_heads[head, q_at, :]
                grads = g_heads[head, q_at, :]
                scores = lax.dot_general(
                    keys, queries, row_contract, preferred_element_type=jnp.float32
                )
                probs = jnp.where(allowed, jnp.exp(scores - log_ref[head, q_place]), 0.0)
                grad_probs = lax.dot_general(
                    values, grads, row_contract, preferred_element_type=jnp.float32
                )
                grad_scores = (probs * (grad_probs - delta[head, q_place])).astype(jnp.bfloat16)
                dv_part = jnp.dot(
                    probs.astype(jnp.bfloat16), grads, preferred_element_type=jnp.float32
                )
                dk_part = jnp.dot(grad_scores, queries, preferred_element_type=jnp.float32)
                dk = dk_part if dk is None else dk + dk_part
                dv = dv_part if dv is None else dv + dv_part
                part = lax.dot_general(
                    grad_scores,
                    k_heads[head, k_at, :],
                    col_contract,
                    preferred_element_type=jnp.float32,
                )
                dq_part = part if dq_part is None else dq_part + part
            dq[q_at, :] += dq_part
            return dk, dv

        diagonal = lax.broadcasted_iota(jnp.int32, (rows, rows), 0) <= lax.broadcasted_iota(
            jnp.int32, (rows, rows), 1
        )
        state = one_block(k_place, (None, None), diagonal)
        dk, dv = lax.fori_loop(
            k_block + 1, blocks, lambda q_block, s: one_block(q_block ^ rank, s, None), state
        )
        gv_ref[k_at, :] = dv.astype(jnp.bfloat16)
        gk_ref[k_at, :] = finish(dk, k_ref[k_at, :], k_at)
        return carry

    lax.fori_loop(0, blocks, key_step, 0)

    def query_finish(block, carry):
        at = pl.ds(pl.multiple_of(block * rows, rows), rows)
        gq_ref[at, :] = finish(dq[at, :] * HEAD_DIM ** (-0.5), q_ref[at, :], at)
        return carry

    lax.fori_loop(0, blocks, query_finish, 0)


def attention_specs(group_rows, pairs, blocks, rows):
    def column(offset):
        return pl.BlockSpec((group_rows, LANES), lambda p, r: (0, offset + p))

    def fixed(shape):
        return pl.BlockSpec(shape, lambda p, r: (0,) * len(shape))

    ins = [
        column(0),
        column(pairs),
        column(2 * pairs),
        fixed((group_rows, LANES)),
        fixed((group_rows, LANES)),
        pl.BlockSpec((1, LANES), lambda p, r: (0, p)),
        fixed((group_rows, 1)),
        fixed((blocks, 1, rows)),
    ]
    logs = pl.BlockSpec((LANES // HEAD_DIM, blocks, 1, rows), lambda p, r: (p, 0, 0, 0))
    return ins, column(0), logs


def attention_forward(rank, projected, tables, scale, id_col, id_row):
    group_rows, width = projected.shape
    head_cols = width // 3
    pairs = head_cols // LANES
    blocks, _, rows = id_row.shape
    per = LANES // HEAD_DIM
    ins, column, logs = attention_specs(group_rows, pairs, blocks, rows)
    return pl.pallas_call(
        attend_kernel,
        out_shape=(
            jax.ShapeDtypeStruct((group_rows, head_cols), jnp.bfloat16),
            jax.ShapeDtypeStruct((pairs * per, blocks, 1, rows), jnp.float32),
        ),
        grid_spec=pltpu.PrefetchScalarGridSpec(
            num_scalar_prefetch=1,
            grid=(pairs,),
            in_specs=ins,
            out_specs=(column, logs),
            scratch_shapes=[
                pltpu.VMEM((per, group_rows, LANES), jnp.bfloat16),
                pltpu.VMEM((group_rows, LANES), jnp.bfloat16),
                pltpu.VMEM((group_rows, 2 * LANES), jnp.bfloat16),
                pltpu.VMEM((per, rows, 2 * LANES), jnp.float32),
            ],
        ),
        name="attend",
        cost_estimate=pl.CostEstimate(flops=18 * 10**9, bytes_accessed=6 * 10**6, transcendentals=0),
    )(rank, projected, projected, projected, *tables, scale, id_col, id_row)


def attention_backward(rank, projected, tables, scale, id_col, id_row, attended, grads, logs_in):
    group_rows, width = projected.shape
    head_cols = width // 3
    pairs = head_cols // LANES
    blocks, _, rows = id_row.shape
    per = LANES // HEAD_DIM
    ins, column, logs = attention_specs(group_rows, pairs, blocks, rows)
    whole = jax.ShapeDtypeStruct((group_rows, head_cols), jnp.bfloat16)
    wide = pltpu.VMEM((per, group_rows, LANES), jnp.bfloat16)
    flat = pltpu.VMEM((group_rows, LANES), jnp.bfloat16)
    return pl.pallas_call(
        attend_back_kernel,
        out_shape=(whole, whole, whole, jax.ShapeDtypeStruct((8, head_cols), jnp.float32)),
        grid_spec=pltpu.PrefetchScalarGridSpec(
            num_scalar_prefetch=1,
            grid=(pairs,),
            in_specs=ins + [column, column, logs],
            out_specs=(column, column, column, pl.BlockSpec((8, LANES), lambda p, r: (0, p))),
            scratch_shapes=[
                wide,
                wide,
                flat,
                flat,
                wide,
                pltpu.VMEM((per, blocks, 1, rows), jnp.float32),
                pltpu.VMEM((group_rows, LANES), jnp.float32),
            ],
        ),
        name="attend_back",
        cost_estimate=pl.CostEstimate(flops=32 * 10**9, bytes_accessed=8 * 10**6, transcendentals=0),
    )(rank, projected, projected, projected, *tables, scale, id_col, id_row, attended, grads, logs_in)


def relative_rows(values, count):
    rank = lax.axis_index("head")
    rows = values.shape[0] // count
    return jnp.concatenate(
        [lax.dynamic_slice_in_dim(values, (rank ^ k) * rows, rows, 0) for k in range(count)],
        axis=0,
    )


def place_tables(seq_ids):
    group_rows = seq_ids.shape[0]
    row_index = jnp.arange(group_rows, dtype=jnp.int32)
    changed = jnp.concatenate([jnp.ones((1,), dtype=bool), seq_ids[1:] != seq_ids[:-1]])
    starts = lax.cummax(jnp.where(changed, row_index, 0), axis=0)
    places = (row_index - starts).astype(jnp.float32)
    lane = jnp.arange(LANES, dtype=jnp.int32)
    half = HEAD_DIM // 2
    frequency = 10000.0 ** (-(2.0 * (lane % half).astype(jnp.float32)) / HEAD_DIM)
    sign = jnp.where(lane % HEAD_DIM < half, -1.0, 1.0)
    doc_ids = jnp.where(seq_ids < group_rows, seq_ids, group_rows + row_index)
    return places, doc_ids, frequency, sign


def bits_of(size):
    return [1 << k for k in range(size.bit_length() - 1)]


def flip(values, axis, bit):
    size = lax.axis_size(axis)
    return lax.ppermute(values, axis, [(k, k ^ bit) for k in range(size)])


def gather_parts(own, axis):
    parts = {0: own}
    for bit in reversed(bits_of(lax.axis_size(axis))):
        for slot in list(parts):
            parts[slot ^ bit] = flip(parts[slot], axis, bit)
    return parts


def scatter_parts(parts, axis):
    for bit in bits_of(lax.axis_size(axis)):
        kept = {}
        for slot in parts:
            if not slot & bit:
                kept[slot] = parts[slot] + flip(
                    parts[slot | bit].astype(jnp.bfloat16), axis, bit
                ).astype(jnp.float32)
        parts = kept
    return parts[0]


def butterfly(values, axis):
    for bit in bits_of(lax.axis_size(axis)):
        values = values + flip(values, axis, bit)
    return values


inner_swap = [(2, 4), (3, 5), (4, 2), (5, 3)]
inner_to_outer = [(2, 0), (3, 1), (4, 6), (5, 7)]
outer_to_inner = [(0, 2), (1, 3), (6, 4), (7, 5)]


def gather_columns(own):
    if lax.axis_size("dp") != 8:
        whole = own
        for bit in reversed(bits_of(lax.axis_size("dp"))):
            whole = jnp.concatenate([whole, flip(whole, "dp", bit)], axis=1)
        return whole
    pair = jnp.concatenate([own, flip(own, "dp", 2)], axis=1)
    near = lax.ppermute(pair, "dp", inner_swap)
    far = near + lax.ppermute(near, "dp", inner_to_outer)
    return jnp.concatenate([pair, far, flip(pair, "dp", 1), flip(far, "dp", 1)], axis=1)


def scatter_columns(low_half, high_half):
    def low(values):
        return values.astype(jnp.bfloat16)

    if lax.axis_size("dp") != 8:
        for bit in bits_of(lax.axis_size("dp")):
            whole = low_half + flip(low(high_half), "dp", bit).astype(jnp.float32)
            middle = whole.shape[1] // 2
            low_half, high_half = whole[:, :middle], whole[:, middle:]
        return whole
    whole = low_half + flip(low(high_half), "dp", 1).astype(jnp.float32)
    middle = whole.shape[1] // 2
    pair, far = whole[:, :middle], whole[:, middle:]
    far = far + lax.ppermute(low(far), "dp", outer_to_inner).astype(jnp.float32)
    pair = pair + lax.ppermute(low(far), "dp", inner_swap).astype(jnp.float32)
    middle = middle // 2
    return pair[:, :middle] + flip(low(pair[:, middle:]), "dp", 2).astype(jnp.float32)


def scatter_rows(whole):
    rank = lax.axis_index("dp")
    for bit in bits_of(lax.axis_size("dp")):
        middle = whole.shape[0] // 2
        upper = (rank & bit) // bit
        sent = lax.dynamic_slice_in_dim(whole, (1 - upper) * middle, middle, 0)
        kept = lax.dynamic_slice_in_dim(whole, upper * middle, middle, 0)
        whole = kept + flip(sent.astype(jnp.bfloat16), "dp", bit).astype(jnp.float32)
    return whole


def gather_rows(own):
    rank = lax.axis_index("dp")
    for bit in reversed(bits_of(lax.axis_size("dp"))):
        other = flip(own, "dp", bit)
        own = jnp.where(
            (rank & bit) > 0,
            jnp.concatenate([other, own], axis=0),
            jnp.concatenate([own, other], axis=0),
        )
    return own


def local(
    tokens,
    w_query,
    w_key,
    w_value,
    w_out,
    s_qk,
    alpha_attn,
    w_gate,
    w_up,
    w_down,
    s_gate,
    s_up,
    alpha_mlp,
    seq_ids,
    counts,
    out_grad,
):
    head_count = lax.axis_size("head")
    head_rank = lax.axis_index("head")
    own_rows, model_width = tokens.shape
    group_rows = own_rows * head_count
    head_cols = w_query.shape[1]
    half_rows = group_rows // 2
    half_slots = [list(range(head_count // 2)), list(range(head_count // 2, head_count))]

    def gather_halves(own):
        parts = gather_parts(own, "head")
        return [jnp.concatenate([parts[k] for k in slots], axis=0) for slots in half_slots]

    def scatter_halves(halves):
        parts = {}
        for values, slots in zip(halves, half_slots):
            for place, slot in enumerate(slots):
                parts[slot] = values[place * own_rows : (place + 1) * own_rows]
        return scatter_parts(parts, "head")

    def halves_of(values):
        return [values[:half_rows], values[half_rows:]]

    group_tokens = jnp.concatenate(gather_halves(tokens), axis=0)
    gate_scale, up_scale = s_gate[None, :], s_up[None, :]
    gate_w = gather_columns((w_gate.astype(jnp.float32) * gate_scale).astype(jnp.bfloat16))
    up_w = gather_columns((w_up.astype(jnp.float32) * up_scale).astype(jnp.bfloat16))
    down_w = gather_columns(w_down)

    places, doc_ids, frequency, sign = place_tables(seq_ids)
    places = relative_rows(places, head_count)
    doc_ids = relative_rows(doc_ids, head_count)
    angles = places[:, None] * frequency[None, :]
    tables = (jnp.cos(angles), jnp.sin(angles) * sign[None, :])
    rank_word = head_rank.astype(jnp.int32).reshape(1)
    id_col = doc_ids[:, None]
    id_row = doc_ids.reshape(head_count, 1, own_rows)
    scale_row = s_qk[None, :]

    projections = jnp.concatenate([w_query, w_key, w_value], axis=1)
    projected = jnp.dot(group_tokens, projections, preferred_element_type=jnp.float32)
    attended, logs = attention_forward(rank_word, projected, tables, scale_row, id_col, id_row)
    attn_mix = scatter_halves(
        [jnp.dot(rows, w_out, preferred_element_type=jnp.float32) for rows in halves_of(attended)]
    )
    residual = tokens.astype(jnp.float32)
    attn_unit = unit_rms(attn_mix)
    first_sum = residual + alpha_attn * (attn_unit - residual)
    after_attn = unit_rms(first_sum)
    mids = gather_halves(after_attn.astype(jnp.bfloat16))

    def forward_units(mid_rows):
        gate_pre = jnp.dot(mid_rows, gate_w, preferred_element_type=jnp.float32)
        up_pre = jnp.dot(mid_rows, up_w, preferred_element_type=jnp.float32)
        inner = (up_pre * jax.nn.silu(gate_pre)).astype(jnp.bfloat16)
        part = lax.dot_general(inner, down_w, row_contract, preferred_element_type=jnp.float32)
        return gate_pre, up_pre, inner, part

    kept = [forward_units(rows) for rows in mids]
    mlp_out = scatter_halves([k[3] for k in kept])
    mlp_unit = unit_rms(mlp_out)
    second_sum = after_attn + alpha_mlp * (mlp_unit - after_attn)
    output = unit_rms(second_sum)
    row_ids = head_rank * own_rows + jnp.arange(own_rows, dtype=jnp.int32)
    live_rows = (row_ids < counts[0]).astype(jnp.float32)
    grad_second = rms_back(second_sum, out_grad * live_rows[:, None])
    alpha_mlp_grad = jnp.sum(grad_second * (mlp_unit - after_attn), axis=0)
    grad_mlps = gather_halves(rms_back(mlp_out, grad_second * alpha_mlp).astype(jnp.bfloat16))

    def backward_units(grad_rows, gate_pre, up_pre):
        gate_sig = jax.nn.sigmoid(gate_pre)
        grad_inner = jnp.dot(grad_rows, down_w, preferred_element_type=jnp.float32)
        up_back = (grad_inner * (gate_pre * gate_sig)).astype(jnp.bfloat16)
        gate_back = (
            grad_inner * up_pre * gate_sig * (1.0 + gate_pre * (1.0 - gate_sig))
        ).astype(jnp.bfloat16)
        grad_mid = lax.dot_general(
            gate_back, gate_w, row_contract, preferred_element_type=jnp.float32
        ) + lax.dot_general(up_back, up_w, row_contract, preferred_element_type=jnp.float32)
        return gate_back, up_back, grad_mid

    backs = [backward_units(rows, k[0], k[1]) for rows, k in zip(grad_mlps, kept)]
    grad_mid = scatter_halves([b[2] for b in backs])
    unit_half = gate_w.shape[1] // 2

    def unit_grads(lefts, rights):
        left = jnp.concatenate(lefts, axis=0)
        right = jnp.concatenate(rights, axis=0)
        return scatter_columns(
            *[
                lax.dot_general(
                    left,
                    right[:, k * unit_half : (k + 1) * unit_half],
                    col_contract,
                    preferred_element_type=jnp.float32,
                )
                for k in range(2)
            ]
        )

    down_grad = unit_grads(grad_mlps, [k[2] for k in kept])
    gate_flat = unit_grads(mids, [b[0] for b in backs])
    up_flat = unit_grads(mids, [b[1] for b in backs])
    gate_scale_grad = jnp.sum(gate_flat * w_gate.astype(jnp.float32), axis=0)
    up_scale_grad = jnp.sum(up_flat * w_up.astype(jnp.float32), axis=0)
    gate_grad = gate_flat * gate_scale
    up_grad = up_flat * up_scale

    grad_after = grad_second * (1.0 - alpha_mlp) + grad_mid
    grad_first = rms_back(first_sum, grad_after)
    alpha_attn_grad = jnp.sum(grad_first * (attn_unit - residual), axis=0)
    grad_mix = rms_back(attn_mix, grad_first * alpha_attn).astype(jnp.bfloat16)
    grad_mix_group = jnp.concatenate(gather_halves(grad_mix), axis=0)
    out_chunk = scatter_rows(
        lax.dot_general(attended, grad_mix_group, col_contract, preferred_element_type=jnp.float32)
    )
    grad_attended = lax.dot_general(
        grad_mix_group, w_out, row_contract, preferred_element_type=jnp.float32
    ).astype(jnp.bfloat16)
    grad_q, grad_k, grad_v, qk_terms = attention_backward(
        rank_word, projected, tables, scale_row, id_col, id_row, attended, grad_attended, logs
    )
    grad_projected = jnp.concatenate([grad_q, grad_k, grad_v], axis=1)
    proj_chunk = scatter_rows(
        lax.dot_general(
            group_tokens, grad_projected, col_contract, preferred_element_type=jnp.float32
        )
    )
    grad_input = scatter_halves(
        [
            lax.dot_general(rows, projections, row_contract, preferred_element_type=jnp.float32)
            for rows in halves_of(grad_projected)
        ]
    ) + grad_first * (1.0 - alpha_attn)
    proj_sum = gather_rows(proj_chunk.astype(jnp.bfloat16)).astype(jnp.float32)
    out_sum = gather_rows(out_chunk.astype(jnp.bfloat16)).astype(jnp.float32)
    alpha_both = butterfly(jnp.stack([alpha_attn_grad, alpha_mlp_grad]), "head")
    qk_row = jnp.sum(qk_terms, axis=0)[None, :]
    alpha_both, qk_row, _ = lax.optimization_barrier((alpha_both, qk_row, grad_q))
    small = butterfly(jnp.concatenate([alpha_both, jnp.pad(qk_row, ((0, 0), (0, model_width - head_cols)))], axis=0), "dp")
    alpha_sum, qk_sum = small[:2], small[2, :head_cols]
    squares = (
        sum(
            jnp.sum(g * g)
            for g in (proj_chunk, out_chunk, down_grad, gate_grad, up_grad, gate_scale_grad, up_scale_grad)
        )
        + jnp.sum(qk_sum * qk_sum) / lax.axis_size("dp")
    )
    square_sum = butterfly(butterfly(jnp.full((8, 128), squares), "dp"), "head")[0, 0]
    grad_norm = jnp.sqrt(square_sum + jnp.sum(alpha_sum * alpha_sum))
    mean_alpha = jnp.mean(jnp.concatenate([alpha_attn, alpha_mlp]))
    return (
        output.astype(jnp.bfloat16),
        grad_input,
        proj_sum[:, :head_cols],
        proj_sum[:, head_cols : 2 * head_cols],
        proj_sum[:, 2 * head_cols :],
        out_sum,
        qk_sum,
        alpha_sum[0],
        gate_grad,
        up_grad,
        down_grad,
        gate_scale_grad,
        up_scale_grad,
        alpha_sum[1],
        grad_norm,
        mean_alpha,
    )


def solution(mesh):
    in_specs = (
        P(("dp", "head"), None),
        P(None, "head"),
        P(None, "head"),
        P(None, "head"),
        P("head", None),
        P("head"),
        P(),
        P(None, ("dp", "head")),
        P(None, ("dp", "head")),
        P(None, ("dp", "head")),
        P(("dp", "head")),
        P(("dp", "head")),
        P(),
        P("dp"),
        P("dp"),
        P(("dp", "head"), None),
    )
    out_specs = (
        P(("dp", "head"), None),
        P(("dp", "head"), None),
        P(None, "head"),
        P(None, "head"),
        P(None, "head"),
        P("head", None),
        P("head"),
        P(),
        P(None, ("dp", "head")),
        P(None, ("dp", "head")),
        P(None, ("dp", "head")),
        P(("dp", "head")),
        P(("dp", "head")),
        P(),
        P(),
        P(),
    )
    return jax.shard_map(local, mesh=mesh, in_specs=in_specs, out_specs=out_specs, check_vma=False)
```

```python
import jax
import jax.numpy as jnp
from jax import lax
from jax.experimental import pallas as pl
from jax.experimental.pallas import tpu as pltpu
from jax.sharding import PartitionSpec as P

HEAD_DIM = 64
LANES = 128


epsilon = 1e-06
row_contract = (((1,), (1,)), ((), ()))
col_contract = (((0,), (0,)), ((), ()))


def unit_rms(values):
    return values * lax.rsqrt(jnp.mean(values * values, axis=-1, keepdims=True) + epsilon)


def rms_back(values, grad_in):
    factor = lax.rsqrt(jnp.mean(values * values, axis=-1, keepdims=True) + epsilon)
    normed = values * factor
    return factor * (grad_in - normed * jnp.mean(grad_in * normed, axis=-1, keepdims=True))


def segment_mean(values, spread):
    upper = values.astype(jnp.bfloat16)
    lower = (values - upper.astype(jnp.float32)).astype(jnp.bfloat16)
    return jnp.dot(upper, spread, preferred_element_type=jnp.float32) + jnp.dot(
        lower, spread, preferred_element_type=jnp.float32
    )


def swap_halves(values):
    lane = lax.broadcasted_iota(jnp.int32, values.shape, 1)
    return jnp.where(
        lane % HEAD_DIM < HEAD_DIM // 2,
        pltpu.roll(values, LANES - HEAD_DIM // 2, 1),
        pltpu.roll(values, HEAD_DIM // 2, 1),
    )


def spread_matrix():
    row = lax.broadcasted_iota(jnp.int32, (LANES, LANES), 0) // HEAD_DIM
    col = lax.broadcasted_iota(jnp.int32, (LANES, LANES), 1) // HEAD_DIM
    return jnp.where(row == col, 1.0 / HEAD_DIM, 0.0).astype(jnp.bfloat16)


def turned_unit(raw, cos_b, sine_b, spread):
    turned = raw * cos_b + swap_halves(raw) * sine_b
    factor = lax.rsqrt(segment_mean(turned * turned, spread) + epsilon)
    return turned * factor, factor


def head_masks(shape):
    lane = lax.broadcasted_iota(jnp.int32, shape, 1)
    return [lane // HEAD_DIM == k for k in range(LANES // HEAD_DIM)]


def attend_kernel(rank_ref, q_ref, k_ref, v_ref, cos_ref, sine_ref, scale_ref, idc_ref, idr_ref,
                  out_ref, log_ref, q_heads, k_all, v_wide, acc):
    blocks, _, rows = idr_ref.shape
    rank = rank_ref[0]
    spread = spread_matrix()
    masks = head_masks((rows, LANES))
    scale = scale_ref[...]

    def prepare(block, carry):
        at = pl.ds(pl.multiple_of(block * rows, rows), rows)
        cos_b, sine_b = cos_ref[at, :], sine_ref[at, :]
        q_unit, _ = turned_unit(q_ref[at, :], cos_b, sine_b, spread)
        k_unit, _ = turned_unit(k_ref[at, :], cos_b, sine_b, spread)
        q_norm = q_unit * scale * HEAD_DIM ** (-0.5)
        for head, mask in enumerate(masks):
            q_heads[head, at, :] = jnp.where(mask, q_norm, 0.0).astype(jnp.bfloat16)
        k_all[at, :] = (k_unit * scale).astype(jnp.bfloat16)
        v_wide[at, :LANES] = v_ref[at, :].astype(jnp.bfloat16)
        v_wide[at, LANES:] = jnp.ones((rows, LANES), jnp.bfloat16)
        return carry

    lax.fori_loop(0, blocks, prepare, 0)
    ones_rows = jnp.ones((8, rows), jnp.bfloat16)

    def query_step(q_block, carry):
        q_place = q_block ^ rank
        q_at = pl.ds(pl.multiple_of(q_place * rows, rows), rows)
        id_col = idc_ref[q_at, :]

        def one_block(k_place, sums, first, extra):
            k_at = pl.ds(pl.multiple_of(k_place * rows, rows), rows)
            keys = k_all[k_at, :]
            values = v_wide[k_at, :]
            allowed = id_col == idr_ref[k_place]
            if extra is not None:
                allowed = allowed & extra
            new_sums = []
            for head in range(len(masks)):
                scores = lax.dot_general(
                    q_heads[head, q_at, :], keys, row_contract, preferred_element_type=jnp.float32
                )
                probs = jnp.where(allowed, jnp.exp(scores), 0.0).astype(jnp.bfloat16)
                part = jnp.dot(probs, values, preferred_element_type=jnp.float32)
                acc[head] = part if first else acc[head] + part
                row_sum = lax.dot_general(
                    ones_rows, probs, row_contract, preferred_element_type=jnp.float32
                )
                new_sums.append(row_sum if first else sums[head] + row_sum)
            return tuple(new_sums)

        diagonal = lax.broadcasted_iota(jnp.int32, (rows, rows), 0) >= lax.broadcasted_iota(
            jnp.int32, (rows, rows), 1
        )
        sums = one_block(q_place, None, True, diagonal)
        sums = lax.fori_loop(
            0, q_block, lambda k_block, s: one_block(k_block ^ rank, s, False, None), sums
        )
        result = acc[0][:, :LANES] / acc[0][:, LANES:]
        for head in range(1, len(masks)):
            result = jnp.where(masks[head], acc[head][:, :LANES] / acc[head][:, LANES:], result)
        out_ref[q_at, :] = result.astype(jnp.bfloat16)
        for head in range(len(masks)):
            log_ref[head, q_place] = jnp.log(sums[head][:1])
        return carry

    lax.fori_loop(0, blocks, query_step, 0)


def attend_back_kernel(rank_ref, q_ref, k_ref, v_ref, cos_ref, sine_ref, scale_ref, idc_ref, idr_ref,
                       out_ref, grad_ref, log_ref,
                       gq_ref, gk_ref, gv_ref, gs_ref,
                       q_heads, k_heads, k_all, v_all, g_heads, delta, dq):
    blocks, _, rows = idr_ref.shape
    heads = LANES // HEAD_DIM
    rank = rank_ref[0]
    spread = spread_matrix()
    masks = head_masks((rows, LANES))
    scale = scale_ref[...]
    lane8 = lax.broadcasted_iota(jnp.int32, (8, LANES), 1) // HEAD_DIM

    def prepare(block, carry):
        at = pl.ds(pl.multiple_of(block * rows, rows), rows)
        cos_b, sine_b = cos_ref[at, :], sine_ref[at, :]
        q_unit, _ = turned_unit(q_ref[at, :], cos_b, sine_b, spread)
        k_unit, _ = turned_unit(k_ref[at, :], cos_b, sine_b, spread)
        q_norm = q_unit * scale * HEAD_DIM ** (-0.5)
        k_norm = k_unit * scale
        grads = grad_ref[at, :]
        product = grads.astype(jnp.float32) * out_ref[at, :].astype(jnp.float32)
        upper = product.astype(jnp.bfloat16)
        lower = (product - upper.astype(jnp.float32)).astype(jnp.bfloat16)
        for head, mask in enumerate(masks):
            q_heads[head, at, :] = jnp.where(mask, q_norm, 0.0).astype(jnp.bfloat16)
            k_heads[head, at, :] = jnp.where(mask, k_norm, 0.0).astype(jnp.bfloat16)
            g_heads[head, at, :] = jnp.where(mask, grads, jnp.zeros_like(grads))
            pick = jnp.where(lane8 == head, 1.0, 0.0).astype(jnp.bfloat16)
            delta[head, block] = (
                lax.dot_general(pick, upper, row_contract, preferred_element_type=jnp.float32)
                + lax.dot_general(pick, lower, row_contract, preferred_element_type=jnp.float32)
            )[:1]
        k_all[at, :] = k_norm.astype(jnp.bfloat16)
        v_all[at, :] = v_ref[at, :].astype(jnp.bfloat16)
        dq[at, :] = jnp.zeros((rows, LANES), jnp.float32)
        return carry

    lax.fori_loop(0, blocks, prepare, 0)
    gs_ref[...] = jnp.zeros(gs_ref.shape, jnp.float32)

    def finish(grad, raw, at):
        cos_b, sine_b = cos_ref[at, :], sine_ref[at, :]
        unit, factor = turned_unit(raw, cos_b, sine_b, spread)
        gs_ref[...] += jnp.sum((grad * unit).reshape(rows // 8, 8, LANES), axis=0)
        grad = grad * scale
        back = factor * (grad - unit * segment_mean(grad * unit, spread))
        return (back * cos_b - swap_halves(back) * sine_b).astype(jnp.bfloat16)

    def key_step(k_block, carry):
        k_place = k_block ^ rank
        k_at = pl.ds(pl.multiple_of(k_place * rows, rows), rows)
        keys = k_all[k_at, :]
        values = v_all[k_at, :]
        id_col = idc_ref[k_at, :]

        def one_block(q_place, state, extra):
            q_at = pl.ds(pl.multiple_of(q_place * rows, rows), rows)
            allowed = id_col == idr_ref[q_place]
            if extra is not None:
                allowed = allowed & extra
            dk, dv = state
            dq_part = None
            for head in range(heads):
                queries = q_heads[head, q_at, :]
                grads = g_heads[head, q_at, :]
                scores = lax.dot_general(
                    keys, queries, row_contract, preferred_element_type=jnp.float32
                )
                probs = jnp.where(allowed, jnp.exp(scores - log_ref[head, q_place]), 0.0)
                grad_probs = lax.dot_general(
                    values, grads, row_contract, preferred_element_type=jnp.float32
                )
                grad_scores = (probs * (grad_probs - delta[head, q_place])).astype(jnp.bfloat16)
                dv_part = jnp.dot(
                    probs.astype(jnp.bfloat16), grads, preferred_element_type=jnp.float32
                )
                dk_part = jnp.dot(grad_scores, queries, preferred_element_type=jnp.float32)
                dk = dk_part if dk is None else dk + dk_part
                dv = dv_part if dv is None else dv + dv_part
                part = lax.dot_general(
                    grad_scores,
                    k_heads[head, k_at, :],
                    col_contract,
                    preferred_element_type=jnp.float32,
                )
                dq_part = part if dq_part is None else dq_part + part
            dq[q_at, :] += dq_part
            return dk, dv

        diagonal = lax.broadcasted_iota(jnp.int32, (rows, rows), 0) <= lax.broadcasted_iota(
            jnp.int32, (rows, rows), 1
        )
        state = one_block(k_place, (None, None), diagonal)
        dk, dv = lax.fori_loop(
            k_block + 1, blocks, lambda q_block, s: one_block(q_block ^ rank, s, None), state
        )
        gv_ref[k_at, :] = dv.astype(jnp.bfloat16)
        gk_ref[k_at, :] = finish(dk, k_ref[k_at, :], k_at)
        return carry

    lax.fori_loop(0, blocks, key_step, 0)

    def query_finish(block, carry):
        at = pl.ds(pl.multiple_of(block * rows, rows), rows)
        gq_ref[at, :] = finish(dq[at, :] * HEAD_DIM ** (-0.5), q_ref[at, :], at)
        return carry

    lax.fori_loop(0, blocks, query_finish, 0)


def attention_specs(group_rows, pairs, blocks, rows, first=0):
    def column(offset):
        return pl.BlockSpec((group_rows, LANES), lambda p, r: (0, offset + first + p))

    def fixed(shape):
        return pl.BlockSpec(shape, lambda p, r: (0,) * len(shape))

    ins = [
        column(0),
        column(pairs),
        column(2 * pairs),
        fixed((group_rows, LANES)),
        fixed((group_rows, LANES)),
        pl.BlockSpec((1, LANES), lambda p, r: (0, first + p)),
        fixed((group_rows, 1)),
        fixed((blocks, 1, rows)),
    ]
    logs = pl.BlockSpec((LANES // HEAD_DIM, blocks, 1, rows), lambda p, r: (first + p, 0, 0, 0))
    return ins, column(0), logs


def attention_forward(rank, projected, tables, scale, id_col, id_row):
    group_rows, width = projected.shape
    head_cols = width // 3
    pairs = head_cols // LANES
    blocks, _, rows = id_row.shape
    per = LANES // HEAD_DIM
    ins, column, logs = attention_specs(group_rows, pairs, blocks, rows)
    return pl.pallas_call(
        attend_kernel,
        out_shape=(
            jax.ShapeDtypeStruct((group_rows, head_cols), jnp.bfloat16),
            jax.ShapeDtypeStruct((pairs * per, blocks, 1, rows), jnp.float32),
        ),
        grid_spec=pltpu.PrefetchScalarGridSpec(
            num_scalar_prefetch=1,
            grid=(pairs,),
            in_specs=ins,
            out_specs=(column, logs),
            scratch_shapes=[
                pltpu.VMEM((per, group_rows, LANES), jnp.bfloat16),
                pltpu.VMEM((group_rows, LANES), jnp.bfloat16),
                pltpu.VMEM((group_rows, 2 * LANES), jnp.bfloat16),
                pltpu.VMEM((per, rows, 2 * LANES), jnp.float32),
            ],
        ),
        name="attend",
        cost_estimate=pl.CostEstimate(flops=18 * 10**9, bytes_accessed=6 * 10**6, transcendentals=0),
    )(rank, projected, projected, projected, *tables, scale, id_col, id_row)


def attention_backward(pair, rank, projected, tables, scale, id_col, id_row, attended, grads, logs_in):
    group_rows, width = projected.shape
    pairs = width // 3 // LANES
    blocks, _, rows = id_row.shape
    per = LANES // HEAD_DIM
    ins, column, logs = attention_specs(group_rows, pairs, blocks, rows, pair)
    whole = jax.ShapeDtypeStruct((group_rows, LANES), jnp.bfloat16)
    block = pl.BlockSpec((group_rows, LANES), lambda p, r: (0, 0))
    wide = pltpu.VMEM((per, group_rows, LANES), jnp.bfloat16)
    flat = pltpu.VMEM((group_rows, LANES), jnp.bfloat16)
    return pl.pallas_call(
        attend_back_kernel,
        out_shape=(whole, whole, whole, jax.ShapeDtypeStruct((8, LANES), jnp.float32)),
        grid_spec=pltpu.PrefetchScalarGridSpec(
            num_scalar_prefetch=1,
            grid=(1,),
            in_specs=ins + [column, column, logs],
            out_specs=(block, block, block, pl.BlockSpec((8, LANES), lambda p, r: (0, 0))),
            scratch_shapes=[
                wide,
                wide,
                flat,
                flat,
                wide,
                pltpu.VMEM((per, blocks, 1, rows), jnp.float32),
                pltpu.VMEM((group_rows, LANES), jnp.float32),
            ],
        ),
        name="attend_back",
        cost_estimate=pl.CostEstimate(flops=16 * 10**9, bytes_accessed=4 * 10**6, transcendentals=0),
    )(rank, projected, projected, projected, *tables, scale, id_col, id_row, attended, grads, logs_in)


def relative_rows(values, count):
    rank = lax.axis_index("head")
    rows = values.shape[0] // count
    return jnp.concatenate(
        [lax.dynamic_slice_in_dim(values, (rank ^ k) * rows, rows, 0) for k in range(count)],
        axis=0,
    )


def place_tables(seq_ids):
    group_rows = seq_ids.shape[0]
    row_index = jnp.arange(group_rows, dtype=jnp.int32)
    changed = jnp.concatenate([jnp.ones((1,), dtype=bool), seq_ids[1:] != seq_ids[:-1]])
    starts = lax.cummax(jnp.where(changed, row_index, 0), axis=0)
    places = (row_index - starts).astype(jnp.float32)
    lane = jnp.arange(LANES, dtype=jnp.int32)
    half = HEAD_DIM // 2
    frequency = 10000.0 ** (-(2.0 * (lane % half).astype(jnp.float32)) / HEAD_DIM)
    sign = jnp.where(lane % HEAD_DIM < half, -1.0, 1.0)
    doc_ids = jnp.where(seq_ids < group_rows, seq_ids, group_rows + row_index)
    return places, doc_ids, frequency, sign


def bits_of(size):
    return [1 << k for k in range(size.bit_length() - 1)]


def flip(values, axis, bit):
    size = lax.axis_size(axis)
    return lax.ppermute(values, axis, [(k, k ^ bit) for k in range(size)])


def gather_parts(own, axis):
    parts = {0: own}
    for bit in reversed(bits_of(lax.axis_size(axis))):
        for slot in list(parts):
            parts[slot ^ bit] = flip(parts[slot], axis, bit)
    return parts


def scatter_parts(parts, axis):
    for bit in bits_of(lax.axis_size(axis)):
        kept = {}
        for slot in parts:
            if not slot & bit:
                kept[slot] = parts[slot] + flip(
                    parts[slot | bit].astype(jnp.bfloat16), axis, bit
                ).astype(jnp.float32)
        parts = kept
    return parts[0]


def butterfly(values, axis):
    for bit in bits_of(lax.axis_size(axis)):
        values = values + flip(values, axis, bit)
    return values


inner_swap = [(2, 4), (3, 5), (4, 2), (5, 3)]


def is_inner():
    place = lax.axis_index("dp") // 2
    return (place == 1) | (place == 2)


def low(values):
    return values.astype(jnp.bfloat16)


def high(values):
    return values.astype(jnp.float32)


def tie(value, anchor):
    if anchor is None:
        return value
    return lax.optimization_barrier((value, anchor))[0]


class Staged:
    def __init__(self, steps):
        self.steps = steps
        self.value = None
        self.sent = next(steps)

    @property
    def done(self):
        return self.value is not None

    def step(self, anchor=None):
        if not self.done:
            try:
                self.sent = self.steps.send(anchor)
            except StopIteration as stop:
                self.value = stop.value
                self.sent = stop.value
        return self.sent

    def finish(self, anchor=None):
        while not self.done:
            anchor = self.step(anchor)
        return self.value


def unit_scatter(left, right, x_first):
    size = lax.axis_size("dp")
    width = right.shape[1] // size

    def part(*places):
        columns = [right[:, a * width : (a + n) * width] for a, n in places]
        return lax.dot_general(
            left,
            columns[0] if len(columns) == 1 else jnp.concatenate(columns, axis=1),
            col_contract,
            preferred_element_type=jnp.float32,
        )

    def cut(values, *places):
        pieces = [values[:, a * width : (a + 1) * width] for a in places]
        return pieces[0] if len(pieces) == 1 else jnp.concatenate(pieces, axis=1)

    if size != 8:
        whole, other = part((0, size // 2)), part((size // 2, size // 2))
        for bit in bits_of(size):
            sent = low(other)
            came = flip(sent, "dp", bit)
            anchor = yield sent
            whole = whole + high(tie(came, anchor))
            middle = whole.shape[1] // 2
            whole, other = whole[:, :middle], whole[:, middle:]
        return jnp.concatenate([whole, other], axis=1)
    if x_first:
        sent = low(part((4, 4)))
        came = flip(sent, "dp", 1)
        anchor = yield sent
        whole = part((0, 4)) + high(tie(came, anchor))
        pair, far = whole[:, : 2 * width], whole[:, 2 * width :]
    else:
        far = part((2, 2), (6, 2))
    sent = low(far)
    came = flip(sent, "dp", 2)
    anchor = yield sent
    far = far + jnp.where(is_inner(), high(tie(came, anchor)), 0.0)
    sent = low(far)
    came = lax.ppermute(sent, "dp", inner_swap)
    anchor = yield sent
    if x_first:
        pair = pair + high(tie(came, anchor))
        sent, kept = low(cut(pair, 1)), cut(pair, 0)
    else:
        pair = part((0, 2), (4, 2)) + high(tie(came, anchor))
        sent, kept = low(cut(pair, 1, 3)), cut(pair, 0, 2)
    came = flip(sent, "dp", 2)
    anchor = yield sent
    kept = kept + high(tie(came, anchor))
    if x_first:
        return kept
    sent, kept = low(cut(kept, 1)), cut(kept, 0)
    came = flip(sent, "dp", 1)
    anchor = yield sent
    return kept + high(tie(came, anchor))


def reduce_rows(whole, bits, chunk):
    rank = lax.axis_index("dp")
    first_row = 0
    for bit in bits:
        middle = whole.shape[0] // 2
        upper = (rank & bit) // bit
        sent = low(lax.dynamic_slice_in_dim(whole, (1 - upper) * middle, middle, 0))
        came = flip(sent, "dp", bit)
        anchor = yield sent
        kept = lax.dynamic_slice_in_dim(whole, upper * middle, middle, 0)
        whole = kept + high(tie(came, anchor))
        first_row = first_row + upper * middle
    chunk.append((whole, first_row))
    own = low(whole)
    for bit in reversed(bits):
        came = flip(own, "dp", bit)
        anchor = yield own
        came = tie(came, anchor)
        own = jnp.where(
            (rank & bit) > 0,
            jnp.concatenate([came, own], axis=0),
            jnp.concatenate([own, came], axis=0),
        )
    return own


def gather_columns(own):
    if lax.axis_size("dp") != 8:
        whole = own
        for bit in reversed(bits_of(lax.axis_size("dp"))):
            whole = jnp.concatenate([whole, flip(whole, "dp", bit)], axis=1)
        return whole
    pair = jnp.concatenate([own, flip(own, "dp", 2)], axis=1)
    near = lax.ppermute(pair, "dp", inner_swap)
    far = jnp.where(is_inner(), near, flip(near, "dp", 2))
    return jnp.concatenate([pair, far, flip(pair, "dp", 1), flip(far, "dp", 1)], axis=1)


def local(
    tokens,
    w_query,
    w_key,
    w_value,
    w_out,
    s_qk,
    alpha_attn,
    w_gate,
    w_up,
    w_down,
    s_gate,
    s_up,
    alpha_mlp,
    seq_ids,
    counts,
    out_grad,
):
    head_count = lax.axis_size("head")
    head_rank = lax.axis_index("head")
    own_rows, model_width = tokens.shape
    group_rows = own_rows * head_count
    head_cols = w_query.shape[1]
    half_rows = group_rows // 2
    half_slots = [list(range(head_count // 2)), list(range(head_count // 2, head_count))]

    def gather_halves(own):
        parts = gather_parts(own, "head")
        return [jnp.concatenate([parts[k] for k in slots], axis=0) for slots in half_slots]

    def scatter_halves(halves):
        parts = {}
        for values, slots in zip(halves, half_slots):
            for place, slot in enumerate(slots):
                parts[slot] = values[place * own_rows : (place + 1) * own_rows]
        return scatter_parts(parts, "head")

    def halves_of(values):
        return [values[:half_rows], values[half_rows:]]

    group_tokens = jnp.concatenate(gather_halves(tokens), axis=0)
    gate_scale, up_scale = s_gate[None, :], s_up[None, :]
    gate_w = gather_columns((w_gate.astype(jnp.float32) * gate_scale).astype(jnp.bfloat16))
    up_w = gather_columns((w_up.astype(jnp.float32) * up_scale).astype(jnp.bfloat16))
    down_w = gather_columns(w_down)

    places, doc_ids, frequency, sign = place_tables(seq_ids)
    places = relative_rows(places, head_count)
    doc_ids = relative_rows(doc_ids, head_count)
    angles = places[:, None] * frequency[None, :]
    tables = (jnp.cos(angles), jnp.sin(angles) * sign[None, :])
    rank_word = head_rank.astype(jnp.int32).reshape(1)
    id_col = doc_ids[:, None]
    id_row = doc_ids.reshape(head_count, 1, own_rows)
    scale_row = s_qk[None, :]

    projections = jnp.concatenate([w_query, w_key, w_value], axis=1)
    projected = jnp.dot(group_tokens, projections, preferred_element_type=jnp.float32)
    attended, logs = attention_forward(rank_word, projected, tables, scale_row, id_col, id_row)
    attn_mix = scatter_halves(
        [jnp.dot(rows, w_out, preferred_element_type=jnp.float32) for rows in halves_of(attended)]
    )
    residual = tokens.astype(jnp.float32)
    attn_unit = unit_rms(attn_mix)
    first_sum = residual + alpha_attn * (attn_unit - residual)
    after_attn = unit_rms(first_sum)
    mids = gather_halves(after_attn.astype(jnp.bfloat16))

    def forward_units(mid_rows):
        gate_pre = jnp.dot(mid_rows, gate_w, preferred_element_type=jnp.float32)
        up_pre = jnp.dot(mid_rows, up_w, preferred_element_type=jnp.float32)
        inner = (up_pre * jax.nn.silu(gate_pre)).astype(jnp.bfloat16)
        part = lax.dot_general(inner, down_w, row_contract, preferred_element_type=jnp.float32)
        return gate_pre, up_pre, inner, part

    kept = [forward_units(rows) for rows in mids]
    mlp_out = scatter_halves([k[3] for k in kept])
    mlp_unit = unit_rms(mlp_out)
    second_sum = after_attn + alpha_mlp * (mlp_unit - after_attn)
    output = unit_rms(second_sum)
    row_ids = head_rank * own_rows + jnp.arange(own_rows, dtype=jnp.int32)
    live_rows = (row_ids < counts[0]).astype(jnp.float32)
    grad_second = rms_back(second_sum, out_grad * live_rows[:, None])
    alpha_mlp_grad = jnp.sum(grad_second * (mlp_unit - after_attn), axis=0)
    grad_mlps = gather_halves(rms_back(mlp_out, grad_second * alpha_mlp).astype(jnp.bfloat16))

    def backward_units(grad_rows, gate_pre, up_pre):
        gate_sig = jax.nn.sigmoid(gate_pre)
        grad_inner = jnp.dot(grad_rows, down_w, preferred_element_type=jnp.float32)
        up_back = (grad_inner * (gate_pre * gate_sig)).astype(jnp.bfloat16)
        gate_back = (
            grad_inner * up_pre * gate_sig * (1.0 + gate_pre * (1.0 - gate_sig))
        ).astype(jnp.bfloat16)
        grad_mid = lax.dot_general(
            gate_back, gate_w, row_contract, preferred_element_type=jnp.float32
        ) + lax.dot_general(up_back, up_w, row_contract, preferred_element_type=jnp.float32)
        return gate_back, up_back, grad_mid

    back0 = backward_units(grad_mlps[0], kept[0][0], kept[0][1])
    grad_mlps[1] = tie(grad_mlps[1], back0[0])
    grad_mlp_all = jnp.concatenate(grad_mlps, axis=0)
    inner_all = jnp.concatenate([k[2] for k in kept], axis=0)
    mid_all = jnp.concatenate(mids, axis=0)
    down_sum = Staged(unit_scatter(grad_mlp_all, inner_all, True))
    back1 = backward_units(tie(grad_mlps[1], down_sum.sent), kept[1][0], kept[1][1])
    backs = [back0, back1]
    grad_mid = scatter_halves([b[2] for b in backs])
    gate_sum = Staged(unit_scatter(mid_all, jnp.concatenate([b[0] for b in backs], axis=0), True))
    up_sum = Staged(unit_scatter(mid_all, jnp.concatenate([b[1] for b in backs], axis=0), False))

    grad_after = grad_second * (1.0 - alpha_mlp) + grad_mid
    grad_first = rms_back(first_sum, grad_after)
    alpha_attn_grad = jnp.sum(grad_first * (attn_unit - residual), axis=0)
    grad_mix = rms_back(attn_mix, grad_first * alpha_attn).astype(jnp.bfloat16)
    grad_mix_group = jnp.concatenate(gather_halves(grad_mix), axis=0)
    alpha_both = butterfly(jnp.stack([alpha_attn_grad, alpha_mlp_grad]), "head")
    down_sum.step(grad_mix)
    grad_attended = lax.dot_general(
        grad_mix_group, w_out, row_contract, preferred_element_type=jnp.float32
    ).astype(jnp.bfloat16)
    out_grad_turned = lax.dot_general(
        grad_mix_group, attended, col_contract, preferred_element_type=jnp.float32
    )
    down_sum.step(grad_attended)
    gate_sum.step(grad_attended)
    up_sum.step(grad_attended)

    chains, chunks, pair_grads = [], [], []
    pairs = head_cols // LANES
    waiting = [down_sum, gate_sum, up_sum]
    extra_rows = 64
    for pair in range(pairs):
        grad_q, grad_k, grad_v, qk_terms = attention_backward(
            pair, rank_word, projected, tables, scale_row, id_col, id_row, attended,
            tie(grad_attended, [chain.sent for chain in waiting]), logs,
        )
        pair_grads.append((grad_q, grad_k, grad_v))
        anchor = grad_q
        whole = lax.dot_general(
            group_tokens,
            jnp.concatenate([grad_q, grad_k, grad_v], axis=1),
            col_contract,
            preferred_element_type=jnp.float32,
        )
        extra = jnp.sum(qk_terms, axis=0)[None, :]
        if pair == 0:
            whole = jnp.concatenate([whole, out_grad_turned], axis=1)
            wide = whole.shape[1]
            alpha_rows = alpha_both.reshape(4, model_width // 2)
            extra = jnp.concatenate(
                [
                    jnp.pad(extra, ((0, 0), (0, wide - LANES))),
                    jnp.pad(alpha_rows, ((0, 0), (0, wide - model_width // 2))),
                ],
                axis=0,
            )
        extra = jnp.pad(
            extra, ((0, extra_rows - extra.shape[0]), (0, whole.shape[1] - extra.shape[1]))
        )
        whole = jnp.concatenate([whole, extra], axis=0)
        chunk = []
        if pair == pairs - 1:
            grad_projected = jnp.concatenate(
                [jnp.concatenate([g[k] for g in pair_grads], axis=1) for k in range(3)], axis=1
            )
            grad_input = scatter_halves(
                [
                    lax.dot_general(rows, projections, row_contract, preferred_element_type=jnp.float32)
                    for rows in halves_of(grad_projected)
                ]
            ) + grad_first * (1.0 - alpha_attn)
        chain = Staged(reduce_rows(whole, bits_of(lax.axis_size("dp")), chunk))
        for other in (down_sum, gate_sum):
            other.step(anchor)
        if pair:
            up_sum.step(anchor)
            for other in chains:
                other.step(anchor)
        chains.append(chain)
        chunks.append(chunk)
        waiting = [down_sum, gate_sum, chain]
    order = chains + [up_sum, gate_sum, down_sum]
    anchor = chains[-1].sent
    while not all(chain.done for chain in order):
        for chain in order:
            if not chain.done:
                anchor = chain.step(anchor)
    down_grad, gate_flat, up_flat = down_sum.value, gate_sum.value, up_sum.value
    gate_scale_grad = jnp.sum(gate_flat * w_gate.astype(jnp.float32), axis=0)
    up_scale_grad = jnp.sum(up_flat * w_up.astype(jnp.float32), axis=0)
    gate_grad = gate_flat * gate_scale
    up_grad = up_flat * up_scale
    squares = sum(
        jnp.sum(g * g) for g in (down_grad, gate_grad, up_grad, gate_scale_grad, up_scale_grad)
    )
    for chunk in chunks:
        values, first_row = chunk[0]
        row = first_row + lax.broadcasted_iota(jnp.int32, values.shape, 0)
        squares += jnp.sum(jnp.where(row <= model_width, values * values, 0.0))
    sums = [high(chain.value) for chain in chains]
    alpha_sum = sums[0][model_width + 1 : model_width + 5, : model_width // 2].reshape(2, model_width)
    qk_sum = jnp.concatenate([s[model_width, :LANES] for s in sums], axis=0)
    weight_grads = [
        jnp.concatenate([s[:model_width, k * LANES : (k + 1) * LANES] for s in sums], axis=1)
        for k in range(3)
    ]
    out_sum = sums[0][:model_width, 3 * LANES :].T
    square_sum = butterfly(butterfly(jnp.full((8, 128), squares), "dp"), "head")[0, 0]
    grad_norm = jnp.sqrt(square_sum + jnp.sum(alpha_sum * alpha_sum))
    mean_alpha = jnp.mean(jnp.concatenate([alpha_attn, alpha_mlp]))
    return (
        output.astype(jnp.bfloat16),
        grad_input,
        *weight_grads,
        out_sum,
        qk_sum,
        alpha_sum[0],
        gate_grad,
        up_grad,
        down_grad,
        gate_scale_grad,
        up_scale_grad,
        alpha_sum[1],
        grad_norm,
        mean_alpha,
    )


def solution(mesh):
    in_specs = (
        P(("dp", "head"), None),
        P(None, "head"),
        P(None, "head"),
        P(None, "head"),
        P("head", None),
        P("head"),
        P(),
        P(None, ("dp", "head")),
        P(None, ("dp", "head")),
        P(None, ("dp", "head")),
        P(("dp", "head")),
        P(("dp", "head")),
        P(),
        P("dp"),
        P("dp"),
        P(("dp", "head"), None),
    )
    out_specs = (
        P(("dp", "head"), None),
        P(("dp", "head"), None),
        P(None, "head"),
        P(None, "head"),
        P(None, "head"),
        P("head", None),
        P("head"),
        P(),
        P(None, ("dp", "head")),
        P(None, ("dp", "head")),
        P(None, ("dp", "head")),
        P(("dp", "head")),
        P(("dp", "head")),
        P(),
        P(),
        P(),
    )
    return jax.shard_map(local, mesh=mesh, in_specs=in_specs, out_specs=out_specs, check_vma=False)
```
